256 devices in a mesh: ab: 64 (over z, y, core), cd: 4 (over x).
Axes of the slice: x: 4, y: 4, z: 8, core: 2. Of those that a mesh axis runs over, the one named last changes fastest.
Arguments:
- t2_amps: float32 [1024, 8192], P('ab', 'cd'), may hold values from -6 to 6
- v_slab: float32 [65536, 8192], P('ab', 'cd'), may hold values from -0.1875 to 0.1875
- ij_irrep: int32 [1024], P('ab'), may hold values from 0 to 7, as said below
- ab_irrep: int32 [65536], P('ab'), may hold values from 0 to 7, as said below
- cd_irrep: int32 [8192], P('cd'), may hold values from 0 to 7, as said below
Outputs:
- ladder: float32 [1024, 65536], P(('ab', 'cd'))
The draws below stay inside these ranges and needn't reach their ends.
Inputs may be any that keep to these rules, and one draw needn't show every extreme that they name: `ij_irrep`: irrep labels of D2h in any order and any counts; a pair couples only to pairs of the same label. All occupied pairs of one device may carry one label. `ab_irrep`: irrep labels of D2h in any order and any counts; all pairs of one device may carry one label. `cd_irrep`: irrep labels of D2h in any order and any counts; all pairs of one device may carry one label.
All inputs are finite; a program needn't handle non-finite values.
Results may differ from the reference program's by a relative error of at most 0.0003.
Values sent between devices are 32-bit elements; how exact they have to be, the bound alone decides.
A program may use at most 64 MiB of HBM per device.

```python
import jax
import jax.numpy as jnp
from jax import lax

AB_DEV = 1024
CD_DEV = 2048
OP = 1024
AB = 65536
CD = 8192
N_AB = 64


def skewed_labels(key, total_pairs, shard_len):
    shards = total_pairs // shard_len
    keys = jax.random.split(key, 5)
    dominant = jax.random.randint(keys[0], (shards,), 0, 8)
    strength = jax.random.randint(keys[1], (shards,), 0, 5)
    chosen = jax.random.randint(keys[2], (), 0, shards)
    strength = jnp.where(jnp.arange(shards) == chosen, 4, strength)
    dice_roll = jax.random.randint(keys[3], (shards, shard_len), 0, 4)
    spread = jax.random.randint(keys[4], (shards, shard_len), 0, 8)
    labels = jnp.where(dice_roll < strength[:, None], dominant[:, None], spread)
    return labels.reshape(total_pairs).astype(jnp.int32)


def draw_ij_irrep(key, part):
    return skewed_labels(jax.random.fold_in(key, 11), OP, OP // (AB // AB_DEV))


def draw_ab_irrep(key, part):
    return skewed_labels(jax.random.fold_in(key, 12), AB, AB_DEV)


def draw_cd_irrep(key, part):
    return skewed_labels(jax.random.fold_in(key, 13), CD, CD_DEV)


def block_levels(stream_key, dims, pieces, low, largest):
    def one(dim, blocks):
        draws = jax.random.uniform(jax.random.fold_in(jax.random.fold_in(stream_key, 6), dim), (blocks,), jnp.float32, low / len(pieces), largest / len(pieces))
        return jnp.repeat(jnp.exp(draws), dims[dim] // blocks).reshape((-1,) + (1,) * (len(dims) - dim - 1))

    loudness = one(*pieces[0])
    for cut in pieces[1:]:
        loudness = loudness * one(*cut)
    return loudness


def normal_values(key, dims, scale, most, pieces=(), held_as=jnp.bfloat16):
    factor_of = block_levels(key, dims, pieces, -0.22, 0.18) if pieces else 1.0
    array = jax.random.normal(key, dims, jnp.float32) * scale * factor_of
    return jnp.minimum(jnp.maximum(array, -most), most).astype(held_as)


def setup_inputs(seed: int = 0) -> dict:
    arg_keys = jax.random.split(jax.random.key(seed), 6)
    return {
        "t2_amps": normal_values(arg_keys[0], (OP, CD), 1.0, 6.0, ((0, 64), (1, 4)), jnp.float32),
        "v_slab": normal_values(arg_keys[1], (AB, CD), (CD // 8) ** -0.5, 0.1875, ((0, 64), (1, 4)), jnp.float32),
        "ij_irrep": draw_ij_irrep(jax.random.fold_in(arg_keys[5], 71), 0),
        "ab_irrep": draw_ab_irrep(jax.random.fold_in(arg_keys[5], 71), 0),
        "cd_irrep": draw_cd_irrep(jax.random.fold_in(arg_keys[5], 71), 0),
    }


def reference(t2_amps, v_slab, ij_irrep, ab_irrep, cd_irrep):
    keep = (ij_irrep[:, None] == cd_irrep[None, :]).astype(t2_amps.dtype)
    t2_sym = t2_amps * keep
    blocks = v_slab.reshape(N_AB, AB_DEV, CD)
    labels = ab_irrep.reshape(N_AB, AB_DEV)

    def one_block(pair):
        v_block, label_block = pair
        v_sym = v_block * (label_block[:, None] == cd_irrep[None, :]).astype(v_block.dtype)
        return lax.dot_general(t2_sym, v_sym, (((1,), (1,)), ((), ())), precision=lax.Precision.HIGHEST, preferred_element_type=jnp.float32)

    parts = lax.map(one_block, (blocks, labels))
    return jnp.transpose(parts, (1, 0, 2)).reshape(OP, AB_DEV * N_AB)
```

```python
import functools

import jax
import jax.numpy as jnp
from jax import lax
from jax.experimental import pallas as pl
from jax.experimental.pallas import tpu as pltpu
from jax.sharding import PartitionSpec as P

NZ, NY, NR, NX = 8, 4, 2, 4
NAB = NZ * NY * NR
ROWS = 16
CD = 2048
AB = 1024
W = CD + 128
LA = 1280
SLOTS = 72
CHUNKS = 2
WIDTH = AB // CHUNKS
HALF = WIDTH // 2
VROWS = 64
F32, BF16 = jnp.float32, jnp.bfloat16
MESH = pl.DeviceIdType.MESH


def pieces():
    size = {"a": LA / 2, "b": (W - LA) / 2}
    free = {}
    queue = []
    order = []

    def issue(now, link, item, amount):
        start = max(free.get(link, 0.0), now)
        free[link] = start + amount / 1000.0
        queue.append((free[link] + 2.0, len(order) + len(queue), link, item))

    def first(now, part, offset, axis):
        for sign in (1, -1):
            issue(now, axis + str(sign), (part, axis, offset, sign, 1), 2 * size[part])

    first(0.0, "a", 0, "z")
    first(0.0, "b", 0, "y")
    first(0.0, "b", 0, "z")
    first(0.0, "a", 0, "y")
    whole = {}
    while queue:
        queue.sort()
        now, _, link, item = queue.pop(0)
        order.append(item)
        part, axis, offset, sign, step = item
        last = 4 if axis == "z" else 2
        if step < last:
            half = step + 1 == last
            issue(now, link, (part, axis, offset, sign, step + 1), size[part] * (1 if half else 2))
        lead = (part == "a") == (axis == "z")
        if lead:
            if step < last:
                first(now, part, -sign * step, "y" if axis == "z" else "z")
            else:
                whole[part] = whole.get(part, 0) + 1
                if whole[part] == 2:
                    first(now, part, last, "y" if axis == "z" else "z")
    return order


ORDER = pieces()
INDEX = {item: n for n, item in enumerate(ORDER)}


def split2(x):
    hi = x.astype(BF16)
    return hi, (x - hi.astype(F32)).astype(BF16)


def dot_nt(a, b):
    return lax.dot_general(a, b, (((1,), (1,)), ((), ())), preferred_element_type=F32)


def column(row):
    n = row.shape[1]
    return jnp.concatenate(
        [jnp.transpose(jnp.broadcast_to(row[:, k : k + 128], (128, 128))) for k in range(0, n, 128)], axis=0
    )


def kernel(
    block_ref, v_ref, ab_ref, cd_ref, out_ref, flag_ref,
    g, vbuf, vhi, vlo, abcol, chi, part, landed, dense, place, tags,
    own_sem, v_sem, recv_sem, send_sem, mate_sem, x_send, x_recv, a_send, a_recv,
):
    ab = lax.axis_index("ab")
    x = lax.axis_index("cd")
    z, y, r = ab // 8, (ab // 2) % 4, ab % 2

    def name(zz, yy, rr):
        return ((zz % NZ) * NY + yy % NY) * NR + rr

    own = pltpu.make_async_copy(block_ref, g.at[ab], own_sem)
    own.start()

    def v_copy(n):
        return pltpu.make_async_copy(v_ref.at[pl.ds(n * VROWS, VROWS)], vbuf.at[n % 3], v_sem.at[n % 3])

    for n in range(2):
        v_copy(n).start()

    barrier = pltpu.get_barrier_semaphore()
    mates = [(name(z + 8 + s, y, r), x) for s in (1, -1)]
    mates += [(name(z, y + 4 + s, r), x) for s in (1, -1)]
    mates += [(name(z, y, 1 - r), x)]
    mates += [(ab, (x + d) % NX) for d in (1, 2, 3)]
    for mate in mates:
        pl.semaphore_signal(barrier, inc=1, device_id=mate, device_id_type=MESH)
    pl.semaphore_wait(barrier, len(mates))
    own.wait()

    lanes = {"a": pl.ds(0, LA), "b": pl.ds(LA, W - LA)}

    def piece(item):
        part_, axis, offset, sign, step = item
        rows = pl.ds(0, ROWS)
        if step == (4 if axis == "z" else 2):
            rows = pl.ds(0, 8) if sign == 1 else pl.ds(8, 8)
        if axis == "z":
            source = name(z + 16 - sign * (step - 1), y + 8 + offset, r)
            target = name(z + 16 + sign, y, r)
        else:
            source = name(z + 16 + offset, y + 8 - sign * (step - 1), r)
            target = name(z, y + 8 + sign, r)
        ref = g.at[source, rows, lanes[part_]]
        return pltpu.make_async_remote_copy(
            src_ref=ref, dst_ref=ref, send_sem=send_sem, recv_sem=recv_sem.at[INDEX[item]],
            device_id=(target, x), device_id_type=MESH,
        )

    def arrived(item):
        part_, axis, offset, sign, step = item
        rows = pl.ds(0, ROWS)
        if step == (4 if axis == "z" else 2):
            rows = pl.ds(0, 8) if sign == 1 else pl.ds(8, 8)
        if axis == "z":
            source = name(z + 16 - sign * step, y + 8 + offset, r)
        else:
            source = name(z + 16 + offset, y + 8 - sign * step, r)
        ref = g.at[source, rows, lanes[part_]]
        pltpu.make_async_copy(ref, ref, recv_sem.at[INDEX[item]]).wait()
        return source, rows

    def give(source, rows, part_):
        ref = g.at[source, rows] if part_ is None else g.at[source, rows, lanes[part_]]
        pltpu.make_async_remote_copy(
            src_ref=ref, dst_ref=ref, send_sem=send_sem, recv_sem=mate_sem,
            device_id=(name(z, y, 1 - r), x), device_id_type=MESH,
        ).start()

    def first(part_, offset, axis):
        for sign in (1, -1):
            piece((part_, axis, offset, sign, 1)).start()

    first("a", 0, "z")
    first("b", 0, "y")
    first("b", 0, "z")
    first("a", 0, "y")
    give(ab, pl.ds(0, ROWS), None)

    ab_row = ab_ref[...]
    cd_row = cd_ref[...]
    abcol[...] = column(ab_row)

    def v_step(n):
        if n + 2 < AB // VROWS:
            v_copy(n + 2).start()
        v_copy(n).wait()
        keep = abcol[n * VROWS : (n + 1) * VROWS, :1] == cd_row
        hi, lo = split2(jnp.where(keep, vbuf[n % 3], 0.0))
        vhi[n * VROWS : (n + 1) * VROWS, :] = hi
        vlo[n * VROWS : (n + 1) * VROWS, :] = lo

    steps = AB // VROWS
    done = 0
    whole = {}
    for count, item in enumerate(ORDER):
        part_, axis, offset, sign, step = item
        source, rows = arrived(item)
        last = 4 if axis == "z" else 2
        if step < last:
            piece((part_, axis, offset, sign, step + 1)).start()
        if (part_ == "a") == (axis == "z"):
            if step < last:
                first(part_, -sign * step, "y" if axis == "z" else "z")
            else:
                whole[part_] = whole.get(part_, 0) + 1
                if whole[part_] == 2:
                    first(part_, last, "y" if axis == "z" else "z")
        give(source, rows, part_)
        while done < steps and done * (len(ORDER) - 16) < count * steps:
            v_step(done)
            done += 1
    while done < steps:
        v_step(done)
        done += 1
    pltpu.make_async_copy(g.at[pl.ds(0, 32)], g.at[pl.ds(0, 32)], mate_sem).wait()

    row_i = lax.broadcasted_iota(jnp.int32, (512, 128), 0)
    lane_i = lax.broadcasted_iota(jnp.int32, (512, 128), 1)
    group = (row_i // 4) % 2
    below = (lax.broadcasted_iota(jnp.int32, (512, 512), 1) < lax.broadcasted_iota(jnp.int32, (512, 512), 0)).astype(BF16)
    slot_no = lax.broadcasted_iota(jnp.int32, (2 * SLOTS, 512), 0).astype(F32)
    cd_f = cd_row.astype(F32)
    most = jnp.zeros((1, 128), F32)
    for p in range(2):
        label = g[:, 8 * p : 8 * p + 8, CD:W].reshape(512, 128)
        one_hot = (label.astype(jnp.int32) + 8 * group == lane_i).astype(F32)
        before = jnp.dot(below, one_hot.astype(BF16), preferred_element_type=F32)
        slot = jnp.broadcast_to(jnp.sum(before * one_hot, axis=1, keepdims=True), (512, 128))
        most = jnp.maximum(most, jnp.max(slot, axis=0, keepdims=True))
        place[p] = slot.reshape(64, 8, 128)
        tags[p] = label.reshape(64, 8, 128)
        spot = jnp.transpose(slot + (SLOTS * group).astype(F32))[:1, :]
        pick = (slot_no == spot).astype(BF16)
        for k in range(0, CD, 512):
            amps = g[:, 8 * p : 8 * p + 8, k : k + 512].reshape(512, 512)
            hi, lo = split2(jnp.where(label[:, :1] == cd_f[:, k : k + 512], amps, 0.0))
            chi[2 * p * SLOTS : 2 * (p + 1) * SLOTS, k : k + 512] = jnp.dot(
                pick, hi, preferred_element_type=F32
            ).astype(BF16)
            chi[(4 + 2 * p) * SLOTS : (6 + 2 * p) * SLOTS, k : k + 512] = jnp.dot(
                pick, lo, preferred_element_type=F32
            ).astype(BF16)
    flag_ref[...] = jnp.broadcast_to(most, (8, 128))

    def x_copy(q, d):
        to = (x + d) % NX
        return pltpu.make_async_remote_copy(
            src_ref=part.at[q, to], dst_ref=landed.at[q, d - 1], send_sem=x_send.at[q, d - 1],
            recv_sem=x_recv.at[q, d - 1], device_id=(ab, to), device_id_type=MESH,
        )

    def product(q):
        cols = slice(q * WIDTH, (q + 1) * WIDTH)
        both = dot_nt(chi[...], vhi[cols, :])
        cross = dot_nt(chi[: 4 * SLOTS, :], vlo[cols, :])
        total = both[: 4 * SLOTS] + both[4 * SLOTS :] + cross
        for c in range(NX):
            part[q, c] = total[c * SLOTS : (c + 1) * SLOTS]
        for d in (2, 1, 3):
            x_copy(q, d).start()

    pair = x // 2
    half_r = lax.broadcasted_iota(jnp.int32, (64, 8, 128), 1) // 4

    def mine(ref):
        t = jnp.where(pair == 1, ref[1], ref[0])
        turned = jnp.concatenate([t[:, 4:, :], t[:, :4, :]], axis=1)
        return jnp.where(half_r == x % 2, t, turned).reshape(512, 128)

    product(0)
    my_slot = mine(place) + (SLOTS * group).astype(F32)
    my_label = mine(tags)
    ab_f = ab_row.astype(F32)
    lane2 = lax.broadcasted_iota(jnp.int32, (512, 2 * SLOTS), 1).astype(F32)
    spread = (my_slot[:, :1] == lane2).astype(BF16)

    def a_copy(q, d):
        dz, dy, dr = d // 8, (d // 2) % 4, d % 2
        to = name(z + dz, y + dy, (r + dr) % 2)
        return pltpu.make_async_remote_copy(
            src_ref=dense.at[q, to], dst_ref=out_ref.at[ab, :, pl.ds(q * HALF, HALF)], send_sem=a_send,
            recv_sem=a_recv, device_id=(to, x), device_id_type=MESH,
        )

    def exchange(q):
        for d in (1, 3, 2):
            x_copy(q, d).wait_recv()
        total = part[q, x] + landed[q, 0] + landed[q, 1] + landed[q, 2]
        even = [total[:, k : k + 128] for k in range(0, WIDTH, 256)]
        odd = [total[:, k + 128 : k + 256] for k in range(0, WIDTH, 256)]
        stacked = jnp.concatenate([jnp.concatenate(even, axis=1), jnp.concatenate(odd, axis=1)], axis=0)
        hi, rest = stacked.astype(BF16), None
        rest = stacked - hi.astype(F32)
        mid, lo = split2(rest)
        rows = jnp.dot(spread, hi, preferred_element_type=F32)
        rows = rows + jnp.dot(spread, mid, preferred_element_type=F32)
        rows = rows + jnp.dot(spread, lo, preferred_element_type=F32)
        base = q * WIDTH
        ab_even = jnp.concatenate([ab_f[:, base + k : base + k + 128] for k in range(0, WIDTH, 256)], axis=1)
        ab_odd = jnp.concatenate([ab_f[:, base + k + 128 : base + k + 256] for k in range(0, WIDTH, 256)], axis=1)
        wanted = jnp.where(group[:, :1] == 0, ab_even, ab_odd)
        rows = jnp.where(my_label[:, :1] == wanted, rows, 0.0)
        dense[q] = rows.reshape(64, 8, HALF)

        def send(d, carry):
            a_copy(q, d).start()
            return carry

        lax.fori_loop(1, NAB, send, 0)
        out_ref[ab, :, q * HALF : (q + 1) * HALF] = dense[q, ab]

    for q in range(CHUNKS):
        if q + 1 < CHUNKS:
            product(q + 1)
        exchange(q)

    for q in range(CHUNKS):
        for d in (1, 2, 3):
            x_copy(q, d).wait_send()
    pltpu.make_async_copy(g.at[pl.ds(0, 63)], g.at[pl.ds(0, 63)], send_sem).wait()
    everything = out_ref.at[pl.ds(0, NAB - 1)]
    pltpu.make_async_copy(everything, everything, a_send).wait()
    pltpu.make_async_copy(everything, everything, a_recv).wait()


def compact(t2_amps, v_slab, ij_irrep, ab_irrep, cd_irrep):
    labels = jnp.broadcast_to(ij_irrep.astype(F32)[:, None], (ROWS, 128))
    block = jnp.concatenate([t2_amps, labels], axis=1)
    vmem = pl.BlockSpec(memory_space=pltpu.VMEM)
    hbm = pl.BlockSpec(memory_space=pl.ANY)
    return pl.pallas_call(
        kernel,
        out_shape=(jax.ShapeDtypeStruct((NAB, 8, AB // 2), F32), jax.ShapeDtypeStruct((8, 128), F32)),
        in_specs=[hbm, hbm, vmem, vmem],
        out_specs=(vmem, vmem),
        scratch_shapes=[
            pltpu.VMEM((NAB, ROWS, W), F32),
            pltpu.VMEM((3, VROWS, CD), F32),
            pltpu.VMEM((AB, CD), BF16),
            pltpu.VMEM((AB, CD), BF16),
            pltpu.VMEM((AB, 128), jnp.int32),
            pltpu.VMEM((8 * SLOTS, CD), BF16),
            pltpu.VMEM((CHUNKS, NX, SLOTS, WIDTH), F32),
            pltpu.VMEM((CHUNKS, NX - 1, SLOTS, WIDTH), F32),
            pltpu.VMEM((CHUNKS, NAB, 8, HALF), F32),
            pltpu.VMEM((2, NAB, 8, 128), F32),
            pltpu.VMEM((2, NAB, 8, 128), F32),
            pltpu.SemaphoreType.DMA,
            pltpu.SemaphoreType.DMA((3,)),
            pltpu.SemaphoreType.DMA((len(ORDER),)),
            pltpu.SemaphoreType.DMA,
            pltpu.SemaphoreType.DMA,
            pltpu.SemaphoreType.DMA((CHUNKS, 3)),
            pltpu.SemaphoreType.DMA((CHUNKS, 3)),
            pltpu.SemaphoreType.DMA,
            pltpu.SemaphoreType.DMA,
        ],
        compiler_params=pltpu.CompilerParams(
            collective_id=0, has_side_effects=True, vmem_limit_bytes=56 * 1024 * 1024
        ),
    )(block, v_slab, ab_irrep[None, :], cd_irrep[None, :])


def dense_path(t2_amps, v_slab, ij_irrep, ab_irrep, cd_irrep):
    t2_sym = t2_amps * (ij_irrep[:, None] == cd_irrep[None, :]).astype(F32)
    v_sym = v_slab * (ab_irrep[:, None] == cd_irrep[None, :]).astype(F32)
    gathered = t2_sym
    hop = 1
    while hop < NAB:
        moved = lax.ppermute(gathered, "ab", [(i, (i + hop) % NAB) for i in range(NAB)])
        gathered = jnp.concatenate([moved, gathered], axis=0)
        hop *= 2
    me, x = lax.axis_index("ab"), lax.axis_index("cd")
    gathered = jnp.roll(gathered, (me + 1) * ROWS, axis=0)
    partial = lax.dot_general(
        gathered, v_sym, (((1,), (1,)), ((), ())), precision=lax.Precision.HIGHEST, preferred_element_type=F32
    )
    parts = jnp.transpose(partial.reshape(NAB, NX, ROWS // NX, AB), (1, 0, 2, 3))
    summed = lax.dynamic_index_in_dim(parts, x, 0, keepdims=False)
    for d in range(1, NX):
        theirs = lax.dynamic_index_in_dim(parts, (x + d) % NX, 0, keepdims=False)
        summed = summed + lax.ppermute(theirs, "cd", [(i, (i + d) % NX) for i in range(NX)])
    return lax.all_to_all(summed.reshape(NAB * ROWS // NX, AB), "ab", split_axis=0, concat_axis=1, tiled=True)


def on_device(t2_amps, v_slab, ij_irrep, ab_irrep, cd_irrep):
    rows, most = compact(t2_amps, v_slab, ij_irrep, ab_irrep, cd_irrep)

    def finish(rows, *_):
        tiles = rows.reshape(NAB, 2, 4, AB // 256, 128)
        return jnp.transpose(tiles, (2, 0, 3, 1, 4)).reshape(4, NAB * AB)

    def dense(_, *args):
        return dense_path(*args)

    return lax.cond(
        most[0, 0] >= SLOTS, dense, finish, rows, t2_amps, v_slab, ij_irrep, ab_irrep, cd_irrep
    )


def solution(mesh):
    in_specs = (P("ab", "cd"), P("ab", "cd"), P("ab"), P("ab"), P("cd"))
    return jax.shard_map(on_device, mesh=mesh, in_specs=in_specs, out_specs=P(("ab", "cd"), None), check_vma=False)
```

```python
import functools

import jax
import jax.numpy as jnp
from jax import lax
from jax.experimental import pallas as pl
from jax.experimental.pallas import tpu as pltpu
from jax.sharding import PartitionSpec as P

NZ, NY, NR, NX = 8, 4, 2, 4
NAB = NZ * NY * NR
ROWS = 16
CD = 2048
AB = 1024
SLOTS = 72
LEAD = 40
CHUNKS = 4
WIDTH = AB // CHUNKS
VROWS = 64
GROUP = NAB * 4
F32, BF16 = jnp.float32, jnp.bfloat16
MESH = pl.DeviceIdType.MESH
EARLY = 10
SPAN = {"a": (0, 24, LEAD), "b": (LEAD, 56, SLOTS)}


def span(part, step, axis, sign):
    low, middle, high = SPAN[part]
    if step < (4 if axis == "z" else 2):
        return low, high - low
    return (low, middle - low) if sign == 1 else (middle, high - middle)


def pieces():
    free = {}
    queue = []
    order = []

    def issue(now, item):
        part, axis, _, sign, step = item
        link = axis + str(sign)
        start = max(free.get(link, 0.0), now)
        free[link] = start + span(part, step, axis, sign)[1] * 0.0111
        queue.append((free[link] + 1.8, len(order) + len(queue), item))

    def first(now, part, offset, axis):
        for sign in (1, -1):
            issue(now, (part, axis, offset, sign, 1))

    first(0.0, "a", 0, "z")
    first(0.0, "b", 0, "y")
    first(0.0, "b", 0, "z")
    first(0.0, "a", 0, "y")
    whole = {}
    while queue:
        queue.sort()
        now, _, item = queue.pop(0)
        order.append(item)
        part, axis, offset, sign, step = item
        last = 4 if axis == "z" else 2
        if step < last:
            issue(now, (part, axis, offset, sign, step + 1))
        if (part == "a") == (axis == "z"):
            if step < last:
                first(now, part, -sign * step, "y" if axis == "z" else "z")
            else:
                whole[part] = whole.get(part, 0) + 1
                if whole[part] == 2:
                    first(now, part, last, "y" if axis == "z" else "z")
    return order


ORDER = pieces()
INDEX = {item: n for n, item in enumerate(ORDER)}


def split2(x):
    hi = x.astype(BF16)
    return hi, (x - hi.astype(F32)).astype(BF16)


def dot_nt(a, b):
    return lax.dot_general(a, b, (((1,), (1,)), ((), ())), preferred_element_type=F32)


def dot(a, b):
    return jnp.dot(a, b, preferred_element_type=F32)


def column(row):
    n = row.shape[1]
    return jnp.concatenate(
        [jnp.transpose(jnp.broadcast_to(row[:, k : k + 128], (128, 128))) for k in range(0, n, 128)], axis=0
    )


def kernel(
    t2_ref, v_ref, ij_ref, ab_ref, cd_ref, chunk_ref, out_ref, flag_ref,
    amps, amps4, mine, labels, rows4, g, vbuf, vhi, vlo, abcol, chi, part, landed, dense,
    own_sem, v_sem, s_send, q_recv, l_recv, recv_sem, send_sem, mate_sem, x_send, x_recv, a_send, a_recv,
):
    ab = lax.axis_index("ab")
    x = lax.axis_index("cd")
    z, y, r = ab // 8, (ab // 2) % 4, ab % 2

    def name(zz, yy, rr):
        return ((zz % NZ) * NY + yy % NY) * NR + rr

    def peer(d):
        return z + d // 8, y + (d // 2) % 4, (r + d % 2) % 2

    load = pltpu.make_async_copy(t2_ref, amps, own_sem.at[0])
    load.start()

    def v_copy(n):
        return pltpu.make_async_copy(v_ref.at[pl.ds(n * VROWS, VROWS)], vbuf.at[n % 3], v_sem.at[n % 3])

    barrier = pltpu.get_barrier_semaphore()

    def greet(d, carry):
        pl.semaphore_signal(barrier, inc=1, device_id=(name(*peer(d)), x), device_id_type=MESH)
        return carry

    lax.fori_loop(1, NAB, greet, 0)
    for d in (1, 2, 3):
        pl.semaphore_signal(barrier, inc=1, device_id=(ab, (x + d) % NX), device_id_type=MESH)

    mine[...] = jnp.full((1, 128), -1, jnp.int32)
    mine[:, :ROWS] = ij_ref[...]
    load.wait()
    for n in range(2):
        v_copy(n).start()
    for c in range(NX):
        amps4[c] = amps[4 * c : 4 * c + 4, :]
    pl.semaphore_wait(barrier, NAB - 1 + NX - 1)

    def scatter(d, carry):
        zz, yy, rr = peer(d)
        zz, yy = zz % NZ, yy % NY
        to = (name(zz, yy, rr), x)
        pltpu.make_async_remote_copy(
            src_ref=mine, dst_ref=labels.at[ab], send_sem=s_send.at[0], recv_sem=l_recv, device_id=to, device_id_type=MESH
        ).start()
        pltpu.make_async_remote_copy(
            src_ref=amps4.at[yy, :, pl.ds(pl.multiple_of((zz * 2 + rr) * 128, 128), 128)], dst_ref=rows4.at[ab],
            send_sem=s_send.at[1], recv_sem=q_recv, device_id=to, device_id_type=MESH,
        ).start()
        return carry

    lax.fori_loop(1, NAB, scatter, 0)
    keep_label = pltpu.make_async_copy(mine, labels.at[ab], own_sem.at[1])
    keep_rows = pltpu.make_async_copy(
        amps4.at[y, :, pl.ds(pl.multiple_of((z * 2 + r) * 128, 128), 128)], rows4.at[ab], own_sem.at[2]
    )
    keep_label.start()
    keep_rows.start()

    ab_row = ab_ref[...]
    cd_row = cd_ref[...]
    abcol[...] = column(ab_row)

    def v_step(n):
        if n + 2 < AB // VROWS:
            v_copy(n + 2).start()
        v_copy(n).wait()
        keep = abcol[n * VROWS : (n + 1) * VROWS, :1] == cd_row
        hi, lo = split2(jnp.where(keep, vbuf[n % 3], 0.0))
        vhi[n * VROWS : (n + 1) * VROWS, :] = hi
        vlo[n * VROWS : (n + 1) * VROWS, :] = lo

    for n in range(EARLY):
        v_step(n)

    row_i = lax.broadcasted_iota(jnp.int32, (GROUP, 128), 0)
    lane_i = lax.broadcasted_iota(jnp.int32, (GROUP, 128), 1)
    square = (GROUP, GROUP)
    below = (lax.broadcasted_iota(jnp.int32, square, 1) < lax.broadcasted_iota(jnp.int32, square, 0)).astype(BF16)
    repeat = (
        lax.broadcasted_iota(jnp.int32, (GROUP, NAB), 1) == lax.broadcasted_iota(jnp.int32, (GROUP, NAB), 0) // 4
    ).astype(BF16)

    keep_label.wait()
    others = pl.ds(0, NAB - 1)
    pltpu.make_async_copy(labels.at[others], labels.at[others], l_recv).wait()
    table = labels[...].reshape(NAB, 128).astype(F32).astype(BF16)
    by_row = dot(repeat, table)

    def slots_of(c):
        label = jnp.sum(jnp.where(lane_i == 4 * c + row_i % 4, by_row, 0.0), axis=1, keepdims=True)
        one_hot = jnp.where(label == lane_i.astype(F32), 1.0, 0.0)
        before = dot(below, one_hot.astype(BF16))
        slot = jnp.sum(before * one_hot, axis=1, keepdims=True)
        return jnp.broadcast_to(label, (GROUP, 128)), jnp.broadcast_to(slot, (GROUP, 128))

    label_y, slot_y = slots_of(y)
    spot = jnp.transpose(slot_y)[:1, :]
    pick = (lax.broadcasted_iota(jnp.int32, (SLOTS, GROUP), 0).astype(F32) == spot).astype(BF16)
    my_cd = chunk_ref[pl.ds(2 * z + r, 1), :].astype(F32)
    keep_rows.wait()
    pltpu.make_async_copy(rows4.at[others], rows4.at[others], q_recv).wait()
    hi, lo = split2(jnp.where(label_y == my_cd, rows4[...].reshape(GROUP, 128), 0.0))
    g[ab] = dot(pick, hi) + dot(pick, lo)

    def sent(item):
        part_, axis, offset, sign, step = item
        low, count = span(part_, step, axis, sign)
        if axis == "z":
            source = name(z + 16 - sign * (step - 1), y + 8 + offset, r)
            target = name(z + 16 + sign, y, r)
        else:
            source = name(z + 16 + offset, y + 8 - sign * (step - 1), r)
            target = name(z, y + 8 + sign, r)
        ref = g.at[source, pl.ds(low, count)]
        return pltpu.make_async_remote_copy(
            src_ref=ref, dst_ref=ref, send_sem=send_sem, recv_sem=recv_sem.at[INDEX[item]],
            device_id=(target, x), device_id_type=MESH,
        )

    def arrived(item):
        part_, axis, offset, sign, step = item
        if axis == "z":
            source = name(z + 16 - sign * step, y + 8 + offset, r)
        else:
            source = name(z + 16 + offset, y + 8 - sign * step, r)
        rows = pl.ds(*span(part_, step, axis, sign))
        ref = g.at[source, rows]
        pltpu.make_async_copy(ref, ref, recv_sem.at[INDEX[item]]).wait()
        return source, rows

    def give(source, rows):
        ref = g.at[source, rows]
        pltpu.make_async_remote_copy(
            src_ref=ref, dst_ref=ref, send_sem=send_sem, recv_sem=mate_sem,
            device_id=(name(z, y, 1 - r), x), device_id_type=MESH,
        ).start()

    def first(part_, offset, axis):
        for sign in (1, -1):
            sent((part_, axis, offset, sign, 1)).start()

    first("a", 0, "z")
    first("b", 0, "y")
    first("b", 0, "z")
    first("a", 0, "y")
    give(ab, pl.ds(0, SLOTS))

    most = jnp.zeros((1, 128), F32)
    my_label = jnp.zeros((GROUP, 128), F32)
    my_slot = jnp.zeros((GROUP, 128), F32)
    for c in range(NX):
        label, slot = slots_of(c)
        most = jnp.maximum(most, jnp.max(slot, axis=0, keepdims=True))
        my_label = jnp.where(x == c, label, my_label)
        my_slot = jnp.where(x == c, slot, my_slot)
    flag_ref[...] = jnp.broadcast_to(most, (8, 128))
    spread = (my_slot[:, :SLOTS] == lane_i[:, :SLOTS].astype(F32)).astype(BF16)

    steps = AB // VROWS
    done = EARLY
    whole = {}
    for count, item in enumerate(ORDER):
        part_, axis, offset, sign, step = item
        source, rows = arrived(item)
        last = 4 if axis == "z" else 2
        if step < last:
            sent((part_, axis, offset, sign, step + 1)).start()
        if (part_ == "a") == (axis == "z"):
            if step < last:
                first(part_, -sign * step, "y" if axis == "z" else "z")
            else:
                whole[part_] = whole.get(part_, 0) + 1
                if whole[part_] == 2:
                    first(part_, last, "y" if axis == "z" else "z")
        give(source, rows)
        while done < steps and (done - EARLY) * (len(ORDER) - 16) < count * (steps - EARLY):
            v_step(done)
            done += 1
    while done < steps:
        v_step(done)
        done += 1
    pltpu.make_async_copy(g.at[pl.ds(0, 32)], g.at[pl.ds(0, 32)], mate_sem).wait()

    for k in range(CD // 128):
        block = jnp.concatenate([g[((k // 2) * NY + c) * NR + k % 2] for c in range(NX)], axis=0)
        hi, lo = split2(block)
        chi[: NX * SLOTS, k * 128 : (k + 1) * 128] = hi
        chi[NX * SLOTS :, k * 128 : (k + 1) * 128] = lo

    def x_copy(q, d):
        to = (x + d) % NX
        return pltpu.make_async_remote_copy(
            src_ref=part.at[q, to], dst_ref=landed.at[q, d - 1], send_sem=x_send.at[q, d - 1],
            recv_sem=x_recv.at[q, d - 1], device_id=(ab, to), device_id_type=MESH,
        )

    def product(q):
        cols = slice(q * WIDTH, (q + 1) * WIDTH)
        both = dot_nt(chi[...], vhi[cols, :])
        cross = dot_nt(chi[: NX * SLOTS, :], vlo[cols, :])
        total = both[: NX * SLOTS] + both[NX * SLOTS :] + cross
        for c in range(NX):
            part[q, c] = total[c * SLOTS : (c + 1) * SLOTS]
        for d in (2, 1, 3):
            x_copy(q, d).start()

    ab_f = ab_row.astype(F32)

    def exchange(q):
        cols = slice(q * WIDTH, (q + 1) * WIDTH)
        for d in (1, 3, 2):
            x_copy(q, d).wait_recv()
        total = part[q, x] + landed[q, 0] + landed[q, 1] + landed[q, 2]
        hi = total.astype(BF16)
        mid, lo = split2(total - hi.astype(F32))
        rows = dot(spread, hi) + dot(spread, mid) + dot(spread, lo)
        rows = jnp.where(my_label[:, :1] == ab_f[:, cols], rows, 0.0)
        dense[q] = rows.reshape(NAB, 4, WIDTH)

        def send(d, carry):
            to = name(*peer(d))
            pltpu.make_async_remote_copy(
                src_ref=dense.at[q, to], dst_ref=out_ref.at[ab, :, pl.ds(q * WIDTH, WIDTH)], send_sem=a_send,
                recv_sem=a_recv, device_id=(to, x), device_id_type=MESH,
            ).start()
            return carry

        lax.fori_loop(1, NAB, send, 0)
        out_ref[ab, :, cols] = dense[q, ab]

    product(0)
    for q in range(CHUNKS):
        if q + 1 < CHUNKS:
            product(q + 1)
        exchange(q)

    for q in range(CHUNKS):
        for d in (1, 2, 3):
            x_copy(q, d).wait_send()
    pltpu.make_async_copy(labels.at[others], labels.at[others], s_send.at[0]).wait()
    pltpu.make_async_copy(rows4.at[others], rows4.at[others], s_send.at[1]).wait()
    pltpu.make_async_copy(g.at[others], g.at[others], send_sem).wait()
    pltpu.make_async_copy(out_ref.at[others], out_ref.at[others], a_send).wait()
    pltpu.make_async_copy(out_ref.at[others], out_ref.at[others], a_recv).wait()


def compact(t2_amps, v_slab, ij_irrep, ab_irrep, cd_irrep):
    vmem = pl.BlockSpec(memory_space=pltpu.VMEM)
    hbm = pl.BlockSpec(memory_space=pl.ANY)
    return pl.pallas_call(
        kernel,
        out_shape=(jax.ShapeDtypeStruct((NAB, 4, AB), F32), jax.ShapeDtypeStruct((8, 128), F32)),
        in_specs=[hbm, hbm, vmem, vmem, vmem, vmem],
        out_specs=(vmem, vmem),
        scratch_shapes=[
            pltpu.VMEM((ROWS, CD), F32),
            pltpu.VMEM((NX, 4, CD), F32),
            pltpu.VMEM((1, 128), jnp.int32),
            pltpu.VMEM((NAB, 1, 128), jnp.int32),
            pltpu.VMEM((NAB, 4, 128), F32),
            pltpu.VMEM((NAB, SLOTS, 128), F32),
            pltpu.VMEM((3, VROWS, CD), F32),
            pltpu.VMEM((AB, CD), BF16),
            pltpu.VMEM((AB, CD), BF16),
            pltpu.VMEM((AB, 128), jnp.int32),
            pltpu.VMEM((2 * NX * SLOTS, CD), BF16),
            pltpu.VMEM((CHUNKS, NX, SLOTS, WIDTH), F32),
            pltpu.VMEM((CHUNKS, NX - 1, SLOTS, WIDTH), F32),
            pltpu.VMEM((CHUNKS, NAB, 4, WIDTH), F32),
            pltpu.SemaphoreType.DMA((3,)),
            pltpu.SemaphoreType.DMA((3,)),
            pltpu.SemaphoreType.DMA((2,)),
            pltpu.SemaphoreType.DMA,
            pltpu.SemaphoreType.DMA,
            pltpu.SemaphoreType.DMA((len(ORDER),)),
            pltpu.SemaphoreType.DMA,
            pltpu.SemaphoreType.DMA,
            pltpu.SemaphoreType.DMA((CHUNKS, 3)),
            pltpu.SemaphoreType.DMA((CHUNKS, 3)),
            pltpu.SemaphoreType.DMA,
            pltpu.SemaphoreType.DMA,
        ],
        compiler_params=pltpu.CompilerParams(
            collective_id=0, has_side_effects=True, vmem_limit_bytes=48 * 1024 * 1024
        ),
    )(t2_amps, v_slab, ij_irrep[None, :], ab_irrep[None, :], cd_irrep[None, :], cd_irrep.reshape(CD // 128, 128))


def dense_path(t2_amps, v_slab, ij_irrep, ab_irrep, cd_irrep):
    t2_sym = t2_amps * (ij_irrep[:, None] == cd_irrep[None, :]).astype(F32)
    v_sym = v_slab * (ab_irrep[:, None] == cd_irrep[None, :]).astype(F32)
    gathered = t2_sym
    hop = 1
    while hop < NAB:
        moved = lax.ppermute(gathered, "ab", [(i, (i + hop) % NAB) for i in range(NAB)])
        gathered = jnp.concatenate([moved, gathered], axis=0)
        hop *= 2
    me, x = lax.axis_index("ab"), lax.axis_index("cd")
    gathered = jnp.roll(gathered, (me + 1) * ROWS, axis=0)
    partial = lax.dot_general(
        gathered, v_sym, (((1,), (1,)), ((), ())), precision=lax.Precision.HIGHEST, preferred_element_type=F32
    )
    parts = jnp.transpose(partial.reshape(NAB, NX, ROWS // NX, AB), (1, 0, 2, 3))
    summed = lax.dynamic_index_in_dim(parts, x, 0, keepdims=False)
    for d in range(1, NX):
        theirs = lax.dynamic_index_in_dim(parts, (x + d) % NX, 0, keepdims=False)
        summed = summed + lax.ppermute(theirs, "cd", [(i, (i + d) % NX) for i in range(NX)])
    return lax.all_to_all(summed.reshape(NAB * ROWS // NX, AB), "ab", split_axis=0, concat_axis=1, tiled=True)


def on_device(t2_amps, v_slab, ij_irrep, ab_irrep, cd_irrep):
    rows, most = compact(t2_amps, v_slab, ij_irrep, ab_irrep, cd_irrep)

    def finish(rows, *_):
        return jnp.transpose(rows, (1, 0, 2)).reshape(4, NAB * AB)

    def dense(_, *args):
        return dense_path(*args)

    return lax.cond(
        most[0, 0] >= SLOTS, dense, finish, rows, t2_amps, v_slab, ij_irrep, ab_irrep, cd_irrep
    )


def solution(mesh):
    in_specs = (P("ab", "cd"), P("ab", "cd"), P("ab"), P("ab"), P("cd"))
    return jax.shard_map(on_device, mesh=mesh, in_specs=in_specs, out_specs=P(("ab", "cd"), None), check_vma=False)
```

```python
import functools

import jax
import jax.numpy as jnp
from jax import lax
from jax.experimental import pallas as pl
from jax.experimental.pallas import tpu as pltpu
from jax.sharding import PartitionSpec as P

NZ, NY, NR, NX = 8, 4, 2, 4
NAB = NZ * NY * NR
ROWS = 16
CD = 2048
AB = 1024
SLOTS = 72
LEAD = 40
WIDTHS = (128, 256, 256, 384)
STARTS = tuple(sum(WIDTHS[:q]) for q in range(len(WIDTHS)))
CHUNKS = len(WIDTHS)
VROWS = 64
GROUP = NAB * 4
F32, BF16 = jnp.float32, jnp.bfloat16
MESH = pl.DeviceIdType.MESH
EARLY = 10
SLOT_TIMES = (30, 38, 46, 54)
SPAN = {"a": (0, 24, LEAD), "b": (LEAD, 56, SLOTS)}
LAST = {"z": 4, "y": 2}
FIRST = {"z": (1, 2), "y": (1, 2)}
HOPS = {("z", 1): 1, ("z", 2): 2, ("z", 3): 1, ("z", 4): 2, ("y", 1): 1, ("y", 2): 2}


def span(part, step, axis, sign):
    low, middle, high = SPAN[part]
    if step < LAST[axis]:
        return low, high - low
    return (low, middle - low) if sign == 1 else (middle, high - middle)


def follow(item, whole):
    part, axis, offset, sign, step = item
    onward = [(part, axis, offset, sign, n) for n in (3, 4)] if (axis, step) == ("z", 2) else []
    turn = None
    if (part == "a") == (axis == "z"):
        if step < LAST[axis]:
            turn = -sign * step
        else:
            whole[part] = whole.get(part, 0) + 1
            if whole[part] == 2:
                turn = LAST[axis]
    return onward, [] if turn is None else opening(part, turn, "y" if axis == "z" else "z")


def opening(part, offset, axis):
    return [(part, axis, offset, sign, step) for step in FIRST[axis] for sign in (1, -1)]


START = opening("a", 0, "z") + opening("b", 0, "y") + opening("b", 0, "z") + opening("a", 0, "y")


def pieces():
    free = {}
    queue = []
    order = []

    def issue(now, item):
        part, axis, _, sign, step = item
        link = axis + str(sign)
        start = max(free.get(link, 0.0), now)
        free[link] = start + span(part, step, axis, sign)[1] * 0.0111 * HOPS[axis, step]
        queue.append((free[link] + 1.1 + 0.7 * HOPS[axis, step], len(order) + len(queue), item))

    for item in START:
        issue(0.0, item)
    whole = {}
    while queue:
        queue.sort()
        now, _, item = queue.pop(0)
        order.append(item)
        for group in follow(item, whole):
            for more in group:
                issue(now, more)
    return order


ORDER = pieces()
INDEX = {item: n for n, item in enumerate(ORDER)}


def split2(x):
    hi = x.astype(BF16)
    return hi, (x - hi.astype(F32)).astype(BF16)


def dot_nt(a, b):
    return lax.dot_general(a, b, (((1,), (1,)), ((), ())), preferred_element_type=F32)


def dot(a, b):
    return jnp.dot(a, b, preferred_element_type=F32)


def column(row):
    n = row.shape[1]
    return jnp.concatenate(
        [jnp.transpose(jnp.broadcast_to(row[:, k : k + 128], (128, 128))) for k in range(0, n, 128)], axis=0
    )


def kernel(
    t2_ref, v_ref, ij_ref, ab_ref, cd_ref, chunk_ref, out_ref, flag_ref,
    amps, amps4, mine, labels, rows4, g, vbuf, vhi, vlo, abcol, chi, part, landed, dense,
    own_sem, v_sem, s_send, q_recv, l_recv, recv_sem, send_sem, mate_sem, x_send, x_recv, a_send, a_recv,
):
    ab = lax.axis_index("ab")
    x = lax.axis_index("cd")
    z, y, r = ab // 8, (ab // 2) % 4, ab % 2

    def name(zz, yy, rr):
        return ((zz % NZ) * NY + yy % NY) * NR + rr

    def peer(d):
        return lax.rem(ab + d, NAB)

    load = pltpu.make_async_copy(t2_ref, amps, own_sem.at[0])
    load.start()

    def v_copy(n):
        return pltpu.make_async_copy(v_ref.at[pl.ds(n * VROWS, VROWS)], vbuf.at[n], v_sem.at[n])

    barrier = pltpu.get_barrier_semaphore()

    def greet(d, carry):
        pl.semaphore_signal(barrier, inc=1, device_id=(peer(d), x), device_id_type=MESH)
        return carry

    lax.fori_loop(1, NAB, greet, 0)
    for d in (1, 2, 3):
        pl.semaphore_signal(barrier, inc=1, device_id=(ab, (x + d) % NX), device_id_type=MESH)

    mine[...] = jnp.full((1, 128), -1, jnp.int32)
    mine[:, :ROWS] = ij_ref[...]
    load.wait()
    for n in range(AB // VROWS):
        v_copy(n).start()
    for to in range(NAB):
        chunk = (to // 8) * 2 + to % 2
        c = (to // 2) % 4
        amps4[to] = amps[4 * c : 4 * c + 4, chunk * 128 : (chunk + 1) * 128]
    pl.semaphore_wait(barrier, NAB - 1 + NX - 1)

    def scatter(d, carry):
        there = peer(d)
        to = (there, x)
        pltpu.make_async_remote_copy(
            src_ref=mine, dst_ref=labels.at[ab], send_sem=s_send.at[0], recv_sem=l_recv, device_id=to, device_id_type=MESH
        ).start()
        pltpu.make_async_remote_copy(
            src_ref=amps4.at[there], dst_ref=rows4.at[ab],
            send_sem=s_send.at[1], recv_sem=q_recv, device_id=to, device_id_type=MESH,
        ).start()
        return carry

    lax.fori_loop(1, NAB, scatter, 0)
    keep_label = pltpu.make_async_copy(mine, labels.at[ab], own_sem.at[1])
    keep_rows = pltpu.make_async_copy(amps4.at[ab], rows4.at[ab], own_sem.at[2])
    keep_label.start()
    keep_rows.start()

    ab_row = ab_ref[...]
    cd_row = cd_ref[...]
    abcol[...] = column(ab_row)

    def v_step(n):
        v_copy(n).wait()
        keep = abcol[n * VROWS : (n + 1) * VROWS, :1] == cd_row
        hi, lo = split2(jnp.where(keep, vbuf[n], 0.0))
        vhi[n * VROWS : (n + 1) * VROWS, :] = hi
        vlo[n * VROWS : (n + 1) * VROWS, :] = lo

    for n in range(EARLY):
        v_step(n)

    row_i = lax.broadcasted_iota(jnp.int32, (GROUP, 128), 0)
    lane_i = lax.broadcasted_iota(jnp.int32, (GROUP, 128), 1)
    square = (GROUP, GROUP)
    below = (lax.broadcasted_iota(jnp.int32, square, 1) < lax.broadcasted_iota(jnp.int32, square, 0)).astype(BF16)
    repeat = (
        lax.broadcasted_iota(jnp.int32, (GROUP, NAB), 1) == lax.broadcasted_iota(jnp.int32, (GROUP, NAB), 0) // 4
    ).astype(BF16)

    keep_label.wait()
    others = pl.ds(0, NAB - 1)
    pltpu.make_async_copy(labels.at[others], labels.at[others], l_recv).wait()
    table = labels[...].reshape(NAB, 128).astype(F32).astype(BF16)
    by_row = dot(repeat, table)

    def slots_of(c):
        label = jnp.sum(jnp.where(lane_i == 4 * c + row_i % 4, by_row, 0.0), axis=1, keepdims=True)
        one_hot = jnp.where(label == lane_i.astype(F32), 1.0, 0.0)
        before = dot(below, one_hot.astype(BF16))
        slot = jnp.sum(before * one_hot, axis=1, keepdims=True)
        return jnp.broadcast_to(label, (GROUP, 128)), jnp.broadcast_to(slot, (GROUP, 128))

    label_y, slot_y = slots_of(y)
    spot = jnp.transpose(slot_y)[:1, :]
    pick = (lax.broadcasted_iota(jnp.int32, (SLOTS, GROUP), 0).astype(F32) == spot).astype(BF16)
    my_cd = chunk_ref[pl.ds(2 * z + r, 1), :].astype(F32)
    keep_rows.wait()
    pltpu.make_async_copy(rows4.at[others], rows4.at[others], q_recv).wait()
    hi, lo = split2(jnp.where(label_y == my_cd, rows4[...].reshape(GROUP, 128), 0.0))
    g[ab] = dot(pick, hi) + dot(pick, lo)

    def sent(item):
        part_, axis, offset, sign, step = item
        low, count = span(part_, step, axis, sign)
        hop = HOPS[axis, step]
        if axis == "z":
            source = name(z + 16 - sign * (step - hop), y + 8 + offset, r)
            target = name(z + 16 + sign * hop, y, r)
        else:
            source = name(z + 16 + offset, y + 8 - sign * (step - hop), r)
            target = name(z, y + 8 + sign * hop, r)
        ref = g.at[source, pl.ds(low, count)]
        return pltpu.make_async_remote_copy(
            src_ref=ref, dst_ref=ref, send_sem=send_sem, recv_sem=recv_sem.at[INDEX[item]],
            device_id=(target, x), device_id_type=MESH,
        )

    def arrived(item):
        part_, axis, offset, sign, step = item
        if axis == "z":
            source = name(z + 16 - sign * step, y + 8 + offset, r)
        else:
            source = name(z + 16 + offset, y + 8 - sign * step, r)
        rows = pl.ds(*span(part_, step, axis, sign))
        ref = g.at[source, rows]
        pltpu.make_async_copy(ref, ref, recv_sem.at[INDEX[item]]).wait()
        return source, rows

    def give(source, rows):
        ref = g.at[source, rows]
        pltpu.make_async_remote_copy(
            src_ref=ref, dst_ref=ref, send_sem=send_sem, recv_sem=mate_sem,
            device_id=(name(z, y, 1 - r), x), device_id_type=MESH,
        ).start()

    for item in START:
        sent(item).start()
    give(ab, pl.ds(0, SLOTS))

    most = jnp.zeros((1, 128), F32)
    my_label = jnp.zeros((GROUP, 128), F32)
    my_slot = jnp.zeros((GROUP, 128), F32)
    steps = AB // VROWS
    done = EARLY
    whole = {}
    for count, item in enumerate(ORDER):
        source, rows = arrived(item)
        for group in follow(item, whole):
            for more in group:
                sent(more).start()
        give(source, rows)
        if count in SLOT_TIMES:
            c = SLOT_TIMES.index(count)
            label, slot = slots_of(c)
            most = jnp.maximum(most, jnp.max(slot, axis=0, keepdims=True))
            my_label = jnp.where(x == c, label, my_label)
            my_slot = jnp.where(x == c, slot, my_slot)
        while done < steps and (done - EARLY) * (len(ORDER) - 16) < count * (steps - EARLY):
            v_step(done)
            done += 1
    while done < steps:
        v_step(done)
        done += 1
    flag_ref[0, 0] = jnp.where(jnp.max(most) >= SLOTS, 1, 0)
    spread = (my_slot[:, :SLOTS] == lane_i[:, :SLOTS].astype(F32)).astype(BF16)
    pltpu.make_async_copy(g.at[pl.ds(0, 32)], g.at[pl.ds(0, 32)], mate_sem).wait()

    for k in range(CD // 128):
        block = jnp.concatenate([g[((k // 2) * NY + c) * NR + k % 2] for c in range(NX)], axis=0)
        hi, lo = split2(block)
        chi[: NX * SLOTS, k * 128 : (k + 1) * 128] = hi
        chi[NX * SLOTS :, k * 128 : (k + 1) * 128] = lo

    def columns(q):
        return pl.ds(STARTS[q], WIDTHS[q])

    def x_copy(q, d):
        to = (x + d) % NX
        return pltpu.make_async_remote_copy(
            src_ref=part.at[to, :, columns(q)], dst_ref=landed.at[d - 1, :, columns(q)], send_sem=x_send.at[q, d - 1],
            recv_sem=x_recv.at[q, d - 1], device_id=(ab, to), device_id_type=MESH,
        )

    def product(q):
        cols = slice(STARTS[q], STARTS[q] + WIDTHS[q])
        both = dot_nt(chi[...], vhi[cols, :])
        cross = dot_nt(chi[: NX * SLOTS, :], vlo[cols, :])
        total = both[: NX * SLOTS] + both[NX * SLOTS :] + cross
        for c in range(NX):
            part[c, :, cols] = total[c * SLOTS : (c + 1) * SLOTS]
        for d in (2, 1, 3):
            x_copy(q, d).start()

    ab_f = ab_row.astype(F32)

    def exchange(q):
        cols = slice(STARTS[q], STARTS[q] + WIDTHS[q])
        for d in (1, 3, 2):
            x_copy(q, d).wait_recv()
        total = part[x, :, cols] + landed[0, :, cols] + landed[1, :, cols] + landed[2, :, cols]
        hi = total.astype(BF16)
        mid, lo = split2(total - hi.astype(F32))
        rows = dot(spread, hi) + dot(spread, mid) + dot(spread, lo)
        rows = jnp.where(my_label[:, :1] == ab_f[:, cols], rows, 0.0)
        dense[:, :, cols] = rows.reshape(NAB, 4, WIDTHS[q])

        def send(d, carry):
            to = peer(d)
            pltpu.make_async_remote_copy(
                src_ref=dense.at[to, :, columns(q)], dst_ref=out_ref.at[ab, :, columns(q)], send_sem=a_send,
                recv_sem=a_recv, device_id=(to, x), device_id_type=MESH,
            ).start()
            return carry

        lax.fori_loop(1, NAB, send, 0)
        out_ref[ab, :, cols] = dense[ab, :, cols]

    product(0)
    for q in range(CHUNKS):
        if q + 1 < CHUNKS:
            product(q + 1)
        exchange(q)

    for q in range(CHUNKS):
        for d in (1, 2, 3):
            x_copy(q, d).wait_send()
    pltpu.make_async_copy(labels.at[others], labels.at[others], s_send.at[0]).wait()
    pltpu.make_async_copy(rows4.at[others], rows4.at[others], s_send.at[1]).wait()
    pltpu.make_async_copy(g.at[others], g.at[others], send_sem).wait()
    pltpu.make_async_copy(out_ref.at[others], out_ref.at[others], a_send).wait()
    pltpu.make_async_copy(out_ref.at[others], out_ref.at[others], a_recv).wait()


def compact(t2_amps, v_slab, ij_irrep, ab_irrep, cd_irrep):
    vmem = pl.BlockSpec(memory_space=pltpu.VMEM)
    hbm = pl.BlockSpec(memory_space=pl.ANY)
    return pl.pallas_call(
        kernel,
        out_shape=(jax.ShapeDtypeStruct((NAB, 4, AB), F32), jax.ShapeDtypeStruct((1, 1), jnp.int32)),
        in_specs=[hbm, hbm, vmem, vmem, vmem, vmem],
        out_specs=(vmem, pl.BlockSpec(memory_space=pltpu.SMEM)),
        scratch_shapes=[
            pltpu.VMEM((ROWS, CD), F32),
            pltpu.VMEM((NAB, 4, 128), F32),
            pltpu.VMEM((1, 128), jnp.int32),
            pltpu.VMEM((NAB, 1, 128), jnp.int32),
            pltpu.VMEM((NAB, 4, 128), F32),
            pltpu.VMEM((NAB, SLOTS, 128), F32),
            pltpu.VMEM((AB // VROWS, VROWS, CD), F32),
            pltpu.VMEM((AB, CD), BF16),
            pltpu.VMEM((AB, CD), BF16),
            pltpu.VMEM((AB, 128), jnp.int32),
            pltpu.VMEM((2 * NX * SLOTS, CD), BF16),
            pltpu.VMEM((NX, SLOTS, AB), F32),
            pltpu.VMEM((NX - 1, SLOTS, AB), F32),
            pltpu.VMEM((NAB, 4, AB), F32),
            pltpu.SemaphoreType.DMA((3,)),
            pltpu.SemaphoreType.DMA((AB // VROWS,)),
            pltpu.SemaphoreType.DMA((2,)),
            pltpu.SemaphoreType.DMA,
            pltpu.SemaphoreType.DMA,
            pltpu.SemaphoreType.DMA((len(ORDER),)),
            pltpu.SemaphoreType.DMA,
            pltpu.SemaphoreType.DMA,
            pltpu.SemaphoreType.DMA((CHUNKS, 3)),
            pltpu.SemaphoreType.DMA((CHUNKS, 3)),
            pltpu.SemaphoreType.DMA,
            pltpu.SemaphoreType.DMA,
        ],
        compiler_params=pltpu.CompilerParams(
            collective_id=0, has_side_effects=True, vmem_limit_bytes=48 * 1024 * 1024
        ),
    )(t2_amps, v_slab, ij_irrep[None, :], ab_irrep[None, :], cd_irrep[None, :], cd_irrep.reshape(CD // 128, 128))


def dense_path(t2_amps, v_slab, ij_irrep, ab_irrep, cd_irrep):
    t2_sym = t2_amps * (ij_irrep[:, None] == cd_irrep[None, :]).astype(F32)
    v_sym = v_slab * (ab_irrep[:, None] == cd_irrep[None, :]).astype(F32)
    gathered = t2_sym
    hop = 1
    while hop < NAB:
        moved = lax.ppermute(gathered, "ab", [(i, (i + hop) % NAB) for i in range(NAB)])
        gathered = jnp.concatenate([moved, gathered], axis=0)
        hop *= 2
    me, x = lax.axis_index("ab"), lax.axis_index("cd")
    gathered = jnp.roll(gathered, (me + 1) * ROWS, axis=0)
    partial = lax.dot_general(
        gathered, v_sym, (((1,), (1,)), ((), ())), precision=lax.Precision.HIGHEST, preferred_element_type=F32
    )
    parts = jnp.transpose(partial.reshape(NAB, NX, ROWS // NX, AB), (1, 0, 2, 3))
    summed = lax.dynamic_index_in_dim(parts, x, 0, keepdims=False)
    for d in range(1, NX):
        theirs = lax.dynamic_index_in_dim(parts, (x + d) % NX, 0, keepdims=False)
        summed = summed + lax.ppermute(theirs, "cd", [(i, (i + d) % NX) for i in range(NX)])
    return lax.all_to_all(summed.reshape(NAB * ROWS // NX, AB), "ab", split_axis=0, concat_axis=1, tiled=True)


def on_device(t2_amps, v_slab, ij_irrep, ab_irrep, cd_irrep):
    rows, over = compact(t2_amps, v_slab, ij_irrep, ab_irrep, cd_irrep)

    def finish(rows, *_):
        return jnp.transpose(rows, (1, 0, 2)).reshape(4, NAB * AB)

    def dense(_, *args):
        return dense_path(*args)

    return lax.cond(
        over[0, 0] > 0, dense, finish, rows, t2_amps, v_slab, ij_irrep, ab_irrep, cd_irrep
    )


def solution(mesh):
    in_specs = (P("ab", "cd"), P("ab", "cd"), P("ab"), P("ab"), P("cd"))
    return jax.shard_map(on_device, mesh=mesh, in_specs=in_specs, out_specs=P(("ab", "cd"), None), check_vma=False)
```

```python
import functools

import jax
import jax.numpy as jnp
from jax import lax
from jax.experimental import pallas as pl
from jax.experimental.pallas import tpu as pltpu
from jax.sharding import PartitionSpec as P

NZ, NY, NR, NX = 8, 4, 2, 4
NAB = NZ * NY * NR
ROWS = 16
CD = 2048
AB = 1024
SLOTS = 72
LEAD = 40
WIDTHS = (128, 256, 256, 384)
STARTS = tuple(sum(WIDTHS[:q]) for q in range(len(WIDTHS)))
CHUNKS = len(WIDTHS)
VROWS = 64
GROUP = NAB * 4
F32, BF16 = jnp.float32, jnp.bfloat16
MESH = pl.DeviceIdType.MESH
EARLY = 10
SLOT_TIMES = (30, 38, 46, 54)
SPAN = {"a": (0, 24, LEAD), "b": (LEAD, 56, SLOTS)}
LAST = {"z": 4, "y": 2}
FIRST = {"z": (1, 2), "y": (1, 2)}
HOPS = {("z", 1): 1, ("z", 2): 2, ("z", 3): 1, ("z", 4): 2, ("y", 1): 1, ("y", 2): 2}


def span(part, step, axis, sign):
    low, middle, high = SPAN[part]
    if step < LAST[axis]:
        return low, high - low
    return (low, middle - low) if sign == 1 else (middle, high - middle)


def follow(item, whole):
    part, axis, offset, sign, step = item
    onward = [(part, axis, offset, sign, n) for n in (3, 4)] if (axis, step) == ("z", 2) else []
    turn = None
    if (part == "a") == (axis == "z"):
        if step < LAST[axis]:
            turn = -sign * step
        else:
            whole[part] = whole.get(part, 0) + 1
            if whole[part] == 2:
                turn = LAST[axis]
    return onward, [] if turn is None else opening(part, turn, "y" if axis == "z" else "z")


def opening(part, offset, axis):
    return [(part, axis, offset, sign, step) for step in FIRST[axis] for sign in (1, -1)]


START = opening("a", 0, "z") + opening("b", 0, "y") + opening("b", 0, "z") + opening("a", 0, "y")


def pieces():
    free = {}
    queue = []
    order = []

    def issue(now, item):
        part, axis, _, sign, step = item
        link = axis + str(sign)
        start = max(free.get(link, 0.0), now)
        free[link] = start + span(part, step, axis, sign)[1] * 0.0111 * HOPS[axis, step]
        queue.append((free[link] + 1.1 + 0.7 * HOPS[axis, step], len(order) + len(queue), item))

    for item in START:
        issue(0.0, item)
    whole = {}
    while queue:
        queue.sort()
        now, _, item = queue.pop(0)
        order.append(item)
        for group in follow(item, whole):
            for more in group:
                issue(now, more)
    return order


ORDER = pieces()
INDEX = {item: n for n, item in enumerate(ORDER)}


def split2(x):
    hi = x.astype(BF16)
    return hi, (x - hi.astype(F32)).astype(BF16)


def dot_nt(a, b):
    return lax.dot_general(a, b, (((1,), (1,)), ((), ())), preferred_element_type=F32)


def dot(a, b):
    return jnp.dot(a, b, preferred_element_type=F32)


def column(row):
    n = row.shape[1]
    return jnp.concatenate(
        [jnp.transpose(jnp.broadcast_to(row[:, k : k + 128], (128, 128))) for k in range(0, n, 128)], axis=0
    )


def kernel(
    t2_ref, v_ref, ij_ref, ab_ref, cd_ref, chunk_ref, out_ref, flag_ref,
    amps, amps4, mine, labels, rows4, g, vbuf, vhi, vlo, abcol, chi, part, landed, dense,
    own_sem, v_sem, s_send, q_recv, l_recv, recv_sem, send_sem, mate_sem, x_send, x_recv, a_send, a_recv,
):
    ab = lax.axis_index("ab")
    x = lax.axis_index("cd")
    z, y, r = ab // 8, (ab // 2) % 4, ab % 2

    def name(zz, yy, rr):
        return ((zz % NZ) * NY + yy % NY) * NR + rr

    def to_all(send):
        send(peer(NAB // 2))

        def two(n, carry):
            send(peer(NAB // 2 - 1 - n))
            send(peer(NAB - (NAB // 2 - 1 - n)))
            return carry

        lax.fori_loop(0, NAB // 2 - 1, two, 0)

    def peer(d):
        return lax.rem(ab + d, NAB)

    load = pltpu.make_async_copy(t2_ref, amps, own_sem.at[0])
    load.start()

    def v_copy(n):
        return pltpu.make_async_copy(v_ref.at[pl.ds(n * VROWS, VROWS)], vbuf.at[n], v_sem.at[n])

    barrier = pltpu.get_barrier_semaphore()

    to_all(lambda there: pl.semaphore_signal(barrier, inc=1, device_id=(there, x), device_id_type=MESH))
    for d in (1, 2, 3):
        pl.semaphore_signal(barrier, inc=1, device_id=(ab, (x + d) % NX), device_id_type=MESH)

    mine[...] = jnp.full((1, 128), -1, jnp.int32)
    mine[:, :ROWS] = ij_ref[...]
    load.wait()
    for n in range(AB // VROWS):
        v_copy(n).start()
    for to in range(NAB):
        chunk = (to // 8) * 2 + to % 2
        c = (to // 2) % 4
        amps4[to] = amps[4 * c : 4 * c + 4, chunk * 128 : (chunk + 1) * 128]
    pl.semaphore_wait(barrier, NAB - 1 + NX - 1)

    def scatter(there):
        to = (there, x)
        pltpu.make_async_remote_copy(
            src_ref=mine, dst_ref=labels.at[ab], send_sem=s_send.at[0], recv_sem=l_recv, device_id=to, device_id_type=MESH
        ).start()
        pltpu.make_async_remote_copy(
            src_ref=amps4.at[there], dst_ref=rows4.at[ab],
            send_sem=s_send.at[1], recv_sem=q_recv, device_id=to, device_id_type=MESH,
        ).start()

    to_all(scatter)
    keep_label = pltpu.make_async_copy(mine, labels.at[ab], own_sem.at[1])
    keep_rows = pltpu.make_async_copy(amps4.at[ab], rows4.at[ab], own_sem.at[2])
    keep_label.start()
    keep_rows.start()

    ab_row = ab_ref[...]
    cd_row = cd_ref[...]
    abcol[...] = column(ab_row)

    def v_step(n):
        v_copy(n).wait()
        keep = abcol[n * VROWS : (n + 1) * VROWS, :1] == cd_row
        hi, lo = split2(jnp.where(keep, vbuf[n], 0.0))
        vhi[n * VROWS : (n + 1) * VROWS, :] = hi
        vlo[n * VROWS : (n + 1) * VROWS, :] = lo

    for n in range(EARLY):
        v_step(n)

    row_i = lax.broadcasted_iota(jnp.int32, (GROUP, 128), 0)
    lane_i = lax.broadcasted_iota(jnp.int32, (GROUP, 128), 1)
    square = (GROUP, GROUP)
    below = (lax.broadcasted_iota(jnp.int32, square, 1) < lax.broadcasted_iota(jnp.int32, square, 0)).astype(BF16)
    repeat = (
        lax.broadcasted_iota(jnp.int32, (GROUP, NAB), 1) == lax.broadcasted_iota(jnp.int32, (GROUP, NAB), 0) // 4
    ).astype(BF16)

    keep_label.wait()
    others = pl.ds(0, NAB - 1)
    pltpu.make_async_copy(labels.at[others], labels.at[others], l_recv).wait()
    table = labels[...].reshape(NAB, 128).astype(F32).astype(BF16)
    by_row = dot(repeat, table)

    def slots_of(c):
        label = jnp.sum(jnp.where(lane_i == 4 * c + row_i % 4, by_row, 0.0), axis=1, keepdims=True)
        one_hot = jnp.where(label == lane_i.astype(F32), 1.0, 0.0)
        before = dot(below, one_hot.astype(BF16))
        slot = jnp.sum(before * one_hot, axis=1, keepdims=True)
        return jnp.broadcast_to(label, (GROUP, 128)), jnp.broadcast_to(slot, (GROUP, 128))

    label_y, slot_y = slots_of(y)
    spot = jnp.transpose(slot_y)[:1, :]
    pick = (lax.broadcasted_iota(jnp.int32, (SLOTS, GROUP), 0).astype(F32) == spot).astype(BF16)
    my_cd = chunk_ref[pl.ds(2 * z + r, 1), :].astype(F32)
    keep_rows.wait()
    pltpu.make_async_copy(rows4.at[others], rows4.at[others], q_recv).wait()
    hi, lo = split2(jnp.where(label_y == my_cd, rows4[...].reshape(GROUP, 128), 0.0))
    g[ab] = dot(pick, hi) + dot(pick, lo)

    def sent(item):
        part_, axis, offset, sign, step = item
        low, count = span(part_, step, axis, sign)
        hop = HOPS[axis, step]
        if axis == "z":
            source = name(z + 16 - sign * (step - hop), y + 8 + offset, r)
            target = name(z + 16 + sign * hop, y, r)
        else:
            source = name(z + 16 + offset, y + 8 - sign * (step - hop), r)
            target = name(z, y + 8 + sign * hop, r)
        ref = g.at[source, pl.ds(low, count)]
        return pltpu.make_async_remote_copy(
            src_ref=ref, dst_ref=ref, send_sem=send_sem, recv_sem=recv_sem.at[INDEX[item]],
            device_id=(target, x), device_id_type=MESH,
        )

    def arrived(item):
        part_, axis, offset, sign, step = item
        if axis == "z":
            source = name(z + 16 - sign * step, y + 8 + offset, r)
        else:
            source = name(z + 16 + offset, y + 8 - sign * step, r)
        rows = pl.ds(*span(part_, step, axis, sign))
        ref = g.at[source, rows]
        pltpu.make_async_copy(ref, ref, recv_sem.at[INDEX[item]]).wait()
        return source, rows

    def give(source, rows):
        ref = g.at[source, rows]
        pltpu.make_async_remote_copy(
            src_ref=ref, dst_ref=ref, send_sem=send_sem, recv_sem=mate_sem,
            device_id=(name(z, y, 1 - r), x), device_id_type=MESH,
        ).start()

    for item in START:
        sent(item).start()
    give(ab, pl.ds(0, SLOTS))

    most = jnp.zeros((1, 128), F32)
    my_label = jnp.zeros((GROUP, 128), F32)
    my_slot = jnp.zeros((GROUP, 128), F32)
    steps = AB // VROWS
    done = EARLY
    whole = {}
    for count, item in enumerate(ORDER):
        source, rows = arrived(item)
        for group in follow(item, whole):
            for more in group:
                sent(more).start()
        give(source, rows)
        if count in SLOT_TIMES:
            c = SLOT_TIMES.index(count)
            label, slot = slots_of(c)
            most = jnp.maximum(most, jnp.max(slot, axis=0, keepdims=True))
            my_label = jnp.where(x == c, label, my_label)
            my_slot = jnp.where(x == c, slot, my_slot)
        while done < steps and (done - EARLY) * (len(ORDER) - 16) < count * (steps - EARLY):
            v_step(done)
            done += 1
    while done < steps:
        v_step(done)
        done += 1
    flag_ref[0, 0] = jnp.where(jnp.max(most) >= SLOTS, 1, 0)
    spread = (my_slot[:, :SLOTS] == lane_i[:, :SLOTS].astype(F32)).astype(BF16)
    pltpu.make_async_copy(g.at[pl.ds(0, 32)], g.at[pl.ds(0, 32)], mate_sem).wait()

    for k in range(CD // 128):
        block = jnp.concatenate([g[((k // 2) * NY + c) * NR + k % 2] for c in range(NX)], axis=0)
        hi, lo = split2(block)
        chi[: NX * SLOTS, k * 128 : (k + 1) * 128] = hi
        chi[NX * SLOTS :, k * 128 : (k + 1) * 128] = lo

    def columns(q):
        return pl.ds(STARTS[q], WIDTHS[q])

    def x_copy(q, d):
        to = (x + d) % NX
        return pltpu.make_async_remote_copy(
            src_ref=part.at[to, :, columns(q)], dst_ref=landed.at[d - 1, :, columns(q)], send_sem=x_send.at[q, d - 1],
            recv_sem=x_recv.at[q, d - 1], device_id=(ab, to), device_id_type=MESH,
        )

    def product(q):
        cols = slice(STARTS[q], STARTS[q] + WIDTHS[q])
        both = dot_nt(chi[...], vhi[cols, :])
        cross = dot_nt(chi[: NX * SLOTS, :], vlo[cols, :])
        total = both[: NX * SLOTS] + both[NX * SLOTS :] + cross
        for c in range(NX):
            part[c, :, cols] = total[c * SLOTS : (c + 1) * SLOTS]
        for d in (2, 1, 3):
            x_copy(q, d).start()

    ab_f = ab_row.astype(F32)

    def exchange(q):
        cols = slice(STARTS[q], STARTS[q] + WIDTHS[q])
        for d in (1, 3, 2):
            x_copy(q, d).wait_recv()
        total = part[x, :, cols] + landed[0, :, cols] + landed[1, :, cols] + landed[2, :, cols]
        hi = total.astype(BF16)
        mid, lo = split2(total - hi.astype(F32))
        rows = dot(spread, hi) + dot(spread, mid) + dot(spread, lo)
        rows = jnp.where(my_label[:, :1] == ab_f[:, cols], rows, 0.0)
        dense[:, :, cols] = rows.reshape(NAB, 4, WIDTHS[q])

        def send(to):
            pltpu.make_async_remote_copy(
                src_ref=dense.at[to, :, columns(q)], dst_ref=out_ref.at[ab, :, columns(q)], send_sem=a_send,
                recv_sem=a_recv, device_id=(to, x), device_id_type=MESH,
            ).start()

        to_all(send)
        out_ref[ab, :, cols] = dense[ab, :, cols]

    product(0)
    for q in range(CHUNKS):
        if q + 1 < CHUNKS:
            product(q + 1)
        exchange(q)

    for q in range(CHUNKS):
        for d in (1, 2, 3):
            x_copy(q, d).wait_send()
    pltpu.make_async_copy(labels.at[others], labels.at[others], s_send.at[0]).wait()
    pltpu.make_async_copy(rows4.at[others], rows4.at[others], s_send.at[1]).wait()
    pltpu.make_async_copy(g.at[others], g.at[others], send_sem).wait()
    pltpu.make_async_copy(out_ref.at[others], out_ref.at[others], a_send).wait()
    pltpu.make_async_copy(out_ref.at[others], out_ref.at[others], a_recv).wait()


def compact(t2_amps, v_slab, ij_irrep, ab_irrep, cd_irrep):
    vmem = pl.BlockSpec(memory_space=pltpu.VMEM)
    hbm = pl.BlockSpec(memory_space=pl.ANY)
    return pl.pallas_call(
        kernel,
        out_shape=(jax.ShapeDtypeStruct((NAB, 4, AB), F32), jax.ShapeDtypeStruct((1, 1), jnp.int32)),
        in_specs=[hbm, hbm, vmem, vmem, vmem, vmem],
        out_specs=(vmem, pl.BlockSpec(memory_space=pltpu.SMEM)),
        scratch_shapes=[
            pltpu.VMEM((ROWS, CD), F32),
            pltpu.VMEM((NAB, 4, 128), F32),
            pltpu.VMEM((1, 128), jnp.int32),
            pltpu.VMEM((NAB, 1, 128), jnp.int32),
            pltpu.VMEM((NAB, 4, 128), F32),
            pltpu.VMEM((NAB, SLOTS, 128), F32),
            pltpu.VMEM((AB // VROWS, VROWS, CD), F32),
            pltpu.VMEM((AB, CD), BF16),
            pltpu.VMEM((AB, CD), BF16),
            pltpu.VMEM((AB, 128), jnp.int32),
            pltpu.VMEM((2 * NX * SLOTS, CD), BF16),
            pltpu.VMEM((NX, SLOTS, AB), F32),
            pltpu.VMEM((NX - 1, SLOTS, AB), F32),
            pltpu.VMEM((NAB, 4, AB), F32),
            pltpu.SemaphoreType.DMA((3,)),
            pltpu.SemaphoreType.DMA((AB // VROWS,)),
            pltpu.SemaphoreType.DMA((2,)),
            pltpu.SemaphoreType.DMA,
            pltpu.SemaphoreType.DMA,
            pltpu.SemaphoreType.DMA((len(ORDER),)),
            pltpu.SemaphoreType.DMA,
            pltpu.SemaphoreType.DMA,
            pltpu.SemaphoreType.DMA((CHUNKS, 3)),
            pltpu.SemaphoreType.DMA((CHUNKS, 3)),
            pltpu.SemaphoreType.DMA,
            pltpu.SemaphoreType.DMA,
        ],
        compiler_params=pltpu.CompilerParams(
            collective_id=0, has_side_effects=True, vmem_limit_bytes=48 * 1024 * 1024
        ),
    )(t2_amps, v_slab, ij_irrep[None, :], ab_irrep[None, :], cd_irrep[None, :], cd_irrep.reshape(CD // 128, 128))


def dense_path(t2_amps, v_slab, ij_irrep, ab_irrep, cd_irrep):
    t2_sym = t2_amps * (ij_irrep[:, None] == cd_irrep[None, :]).astype(F32)
    v_sym = v_slab * (ab_irrep[:, None] == cd_irrep[None, :]).astype(F32)
    gathered = t2_sym
    hop = 1
    while hop < NAB:
        moved = lax.ppermute(gathered, "ab", [(i, (i + hop) % NAB) for i in range(NAB)])
        gathered = jnp.concatenate([moved, gathered], axis=0)
        hop *= 2
    me, x = lax.axis_index("ab"), lax.axis_index("cd")
    gathered = jnp.roll(gathered, (me + 1) * ROWS, axis=0)
    partial = lax.dot_general(
        gathered, v_sym, (((1,), (1,)), ((), ())), precision=lax.Precision.HIGHEST, preferred_element_type=F32
    )
    parts = jnp.transpose(partial.reshape(NAB, NX, ROWS // NX, AB), (1, 0, 2, 3))
    summed = lax.dynamic_index_in_dim(parts, x, 0, keepdims=False)
    for d in range(1, NX):
        theirs = lax.dynamic_index_in_dim(parts, (x + d) % NX, 0, keepdims=False)
        summed = summed + lax.ppermute(theirs, "cd", [(i, (i + d) % NX) for i in range(NX)])
    return lax.all_to_all(summed.reshape(NAB * ROWS // NX, AB), "ab", split_axis=0, concat_axis=1, tiled=True)


def on_device(t2_amps, v_slab, ij_irrep, ab_irrep, cd_irrep):
    rows, over = compact(t2_amps, v_slab, ij_irrep, ab_irrep, cd_irrep)

    def finish(rows, *_):
        return jnp.transpose(rows, (1, 0, 2)).reshape(4, NAB * AB)

    def dense(_, *args):
        return dense_path(*args)

    return lax.cond(
        over[0, 0] > 0, dense, finish, rows, t2_amps, v_slab, ij_irrep, ab_irrep, cd_irrep
    )


def solution(mesh):
    in_specs = (P("ab", "cd"), P("ab", "cd"), P("ab"), P("ab"), P("cd"))
    return jax.shard_map(on_device, mesh=mesh, in_specs=in_specs, out_specs=P(("ab", "cd"), None), check_vma=False)
```

```python
import functools

import jax
import jax.numpy as jnp
from jax import lax
from jax.experimental import pallas as pl
from jax.experimental.pallas import tpu as pltpu
from jax.sharding import PartitionSpec as P

NZ, NY, NR, NX = 8, 4, 2, 4
NAB = NZ * NY * NR
ROWS = 16
CD = 2048
AB = 1024
SLOTS = 72
LEAD = 40
WIDTHS = (128, 256, 384, 256)
STARTS = tuple(sum(WIDTHS[:q]) for q in range(len(WIDTHS)))
CHUNKS = len(WIDTHS)
VROWS = 64
GROUP = NAB * 4
F32, BF16 = jnp.float32, jnp.bfloat16
MESH = pl.DeviceIdType.MESH
EARLY = 10
SLOT_TIMES = (30, 38, 46, 54)
SPAN = {"a": (0, 24, LEAD), "b": (LEAD, 56, SLOTS)}
LAST = {"z": 4, "y": 2}
FIRST = {"z": (1, 2), "y": (1, 2)}
HOPS = {("z", 1): 1, ("z", 2): 2, ("z", 3): 1, ("z", 4): 2, ("y", 1): 1, ("y", 2): 2}


def span(part, step, axis, sign):
    low, middle, high = SPAN[part]
    if step < LAST[axis]:
        return low, high - low
    return (low, middle - low) if sign == 1 else (middle, high - middle)


def follow(item, whole):
    part, axis, offset, sign, step = item
    onward = [(part, axis, offset, sign, n) for n in (3, 4)] if (axis, step) == ("z", 2) else []
    turn = None
    if (part == "a") == (axis == "z"):
        if step < LAST[axis]:
            turn = -sign * step
        else:
            whole[part] = whole.get(part, 0) + 1
            if whole[part] == 2:
                turn = LAST[axis]
    return onward, [] if turn is None else opening(part, turn, "y" if axis == "z" else "z")


def opening(part, offset, axis):
    return [(part, axis, offset, sign, step) for step in FIRST[axis] for sign in (1, -1)]


START = opening("a", 0, "z") + opening("b", 0, "y") + opening("b", 0, "z") + opening("a", 0, "y")


def pieces():
    free = {}
    queue = []
    order = []

    def issue(now, item):
        part, axis, _, sign, step = item
        link = axis + str(sign)
        start = max(free.get(link, 0.0), now)
        free[link] = start + span(part, step, axis, sign)[1] * 0.0111 * HOPS[axis, step]
        queue.append((free[link] + 1.1 + 0.7 * HOPS[axis, step], len(order) + len(queue), item))

    for item in START:
        issue(0.0, item)
    whole = {}
    while queue:
        queue.sort()
        now, _, item = queue.pop(0)
        order.append(item)
        for group in follow(item, whole):
            for more in group:
                issue(now, more)
    return order


ORDER = pieces()
INDEX = {item: n for n, item in enumerate(ORDER)}


def split2(x):
    hi = x.astype(BF16)
    return hi, (x - hi.astype(F32)).astype(BF16)


def dot_nt(a, b):
    return lax.dot_general(a, b, (((1,), (1,)), ((), ())), preferred_element_type=F32)


def dot(a, b):
    return jnp.dot(a, b, preferred_element_type=F32)


def column(row):
    n = row.shape[1]
    return jnp.concatenate(
        [jnp.transpose(jnp.broadcast_to(row[:, k : k + 128], (128, 128))) for k in range(0, n, 128)], axis=0
    )


def kernel(
    t2_ref, v_ref, ij_ref, ab_ref, cd_ref, chunk_ref, out_ref, flag_ref,
    amps, amps4, mine, labels, rows4, g, vbuf, vhi, vlo, abcol, chi, part, landed, dense,
    own_sem, v_sem, s_send, q_recv, l_recv, recv_sem, send_sem, mate_sem, x_send, x_recv, a_send, a_recv,
):
    ab = lax.axis_index("ab")
    x = lax.axis_index("cd")
    z, y, r = ab // 8, (ab // 2) % 4, ab % 2

    def name(zz, yy, rr):
        return ((zz % NZ) * NY + yy % NY) * NR + rr

    def to_all(send):
        send(peer(NAB // 2))

        def two(n, carry):
            send(peer(NAB // 2 - 1 - n))
            send(peer(NAB - (NAB // 2 - 1 - n)))
            return carry

        lax.fori_loop(0, NAB // 2 - 1, two, 0)

    def peer(d):
        return lax.rem(ab + d, NAB)

    load = pltpu.make_async_copy(t2_ref, amps, own_sem.at[0])
    load.start()

    def v_copy(n):
        return pltpu.make_async_copy(v_ref.at[pl.ds(n * VROWS, VROWS)], vbuf.at[n], v_sem.at[n])

    barrier = pltpu.get_barrier_semaphore()

    to_all(lambda there: pl.semaphore_signal(barrier, inc=1, device_id=(there, x), device_id_type=MESH))
    for d in (1, 2, 3):
        pl.semaphore_signal(barrier, inc=1, device_id=(ab, (x + d) % NX), device_id_type=MESH)

    mine[...] = jnp.full((1, 128), -1, jnp.int32)
    mine[:, :ROWS] = ij_ref[...]
    load.wait()
    for n in range(AB // VROWS):
        v_copy(n).start()
    for to in range(NAB):
        chunk = (to // 8) * 2 + to % 2
        c = (to // 2) % 4
        amps4[to] = amps[4 * c : 4 * c + 4, chunk * 128 : (chunk + 1) * 128]
    pl.semaphore_wait(barrier, NAB - 1 + NX - 1)

    def scatter(there):
        to = (there, x)
        pltpu.make_async_remote_copy(
            src_ref=mine, dst_ref=labels.at[ab], send_sem=s_send.at[0], recv_sem=l_recv, device_id=to, device_id_type=MESH
        ).start()
        pltpu.make_async_remote_copy(
            src_ref=amps4.at[there], dst_ref=rows4.at[ab],
            send_sem=s_send.at[1], recv_sem=q_recv, device_id=to, device_id_type=MESH,
        ).start()

    to_all(scatter)
    keep_label = pltpu.make_async_copy(mine, labels.at[ab], own_sem.at[1])
    keep_rows = pltpu.make_async_copy(amps4.at[ab], rows4.at[ab], own_sem.at[2])
    keep_label.start()
    keep_rows.start()

    ab_row = ab_ref[...]
    cd_row = cd_ref[...]
    abcol[...] = column(ab_row)

    def v_step(n):
        v_copy(n).wait()
        keep = abcol[n * VROWS : (n + 1) * VROWS, :1] == cd_row
        hi, lo = split2(jnp.where(keep, vbuf[n], 0.0))
        vhi[n * VROWS : (n + 1) * VROWS, :] = hi
        vlo[n * VROWS : (n + 1) * VROWS, :] = lo

    for n in range(EARLY):
        v_step(n)

    row_i = lax.broadcasted_iota(jnp.int32, (GROUP, 128), 0)
    lane_i = lax.broadcasted_iota(jnp.int32, (GROUP, 128), 1)
    square = (GROUP, GROUP)
    below = (lax.broadcasted_iota(jnp.int32, square, 1) < lax.broadcasted_iota(jnp.int32, square, 0)).astype(BF16)
    repeat = (
        lax.broadcasted_iota(jnp.int32, (GROUP, NAB), 1) == lax.broadcasted_iota(jnp.int32, (GROUP, NAB), 0) // 4
    ).astype(BF16)

    keep_label.wait()
    others = pl.ds(0, NAB - 1)
    pltpu.make_async_copy(labels.at[others], labels.at[others], l_recv).wait()
    table = labels[...].reshape(NAB, 128).astype(F32).astype(BF16)
    by_row = dot(repeat, table)

    def slots_of(c):
        label = jnp.sum(jnp.where(lane_i == 4 * c + row_i % 4, by_row, 0.0), axis=1, keepdims=True)
        one_hot = jnp.where(label == lane_i.astype(F32), 1.0, 0.0)
        before = dot(below, one_hot.astype(BF16))
        slot = jnp.sum(before * one_hot, axis=1, keepdims=True)
        return jnp.broadcast_to(label, (GROUP, 128)), jnp.broadcast_to(slot, (GROUP, 128))

    label_y, slot_y = slots_of(y)
    spot = jnp.transpose(slot_y)[:1, :]
    pick = (lax.broadcasted_iota(jnp.int32, (SLOTS, GROUP), 0).astype(F32) == spot).astype(BF16)
    my_cd = chunk_ref[pl.ds(2 * z + r, 1), :].astype(F32)
    keep_rows.wait()
    pltpu.make_async_copy(rows4.at[others], rows4.at[others], q_recv).wait()
    hi, lo = split2(jnp.where(label_y == my_cd, rows4[...].reshape(GROUP, 128), 0.0))
    g[ab] = dot(pick, hi) + dot(pick, lo)

    def sent(item):
        part_, axis, offset, sign, step = item
        low, count = span(part_, step, axis, sign)
        hop = HOPS[axis, step]
        if axis == "z":
            source = name(z + 16 - sign * (step - hop), y + 8 + offset, r)
            target = name(z + 16 + sign * hop, y, r)
        else:
            source = name(z + 16 + offset, y + 8 - sign * (step - hop), r)
            target = name(z, y + 8 + sign * hop, r)
        ref = g.at[source, pl.ds(low, count)]
        return pltpu.make_async_remote_copy(
            src_ref=ref, dst_ref=ref, send_sem=send_sem, recv_sem=recv_sem.at[INDEX[item]],
            device_id=(target, x), device_id_type=MESH,
        )

    def arrived(item):
        part_, axis, offset, sign, step = item
        if axis == "z":
            source = name(z + 16 - sign * step, y + 8 + offset, r)
        else:
            source = name(z + 16 + offset, y + 8 - sign * step, r)
        rows = pl.ds(*span(part_, step, axis, sign))
        ref = g.at[source, rows]
        pltpu.make_async_copy(ref, ref, recv_sem.at[INDEX[item]]).wait()
        return source, rows

    def give(source, rows):
        ref = g.at[source, rows]
        pltpu.make_async_remote_copy(
            src_ref=ref, dst_ref=ref, send_sem=send_sem, recv_sem=mate_sem,
            device_id=(name(z, y, 1 - r), x), device_id_type=MESH,
        ).start()

    for item in START:
        sent(item).start()
    give(ab, pl.ds(0, SLOTS))

    most = jnp.zeros((1, 128), F32)
    my_label = jnp.zeros((GROUP, 128), F32)
    my_slot = jnp.zeros((GROUP, 128), F32)
    steps = AB // VROWS
    done = EARLY
    whole = {}
    for count, item in enumerate(ORDER):
        source, rows = arrived(item)
        for group in follow(item, whole):
            for more in group:
                sent(more).start()
        give(source, rows)
        if count in SLOT_TIMES:
            c = SLOT_TIMES.index(count)
            label, slot = slots_of(c)
            most = jnp.maximum(most, jnp.max(slot, axis=0, keepdims=True))
            my_label = jnp.where(x == c, label, my_label)
            my_slot = jnp.where(x == c, slot, my_slot)
        while done < steps and (done - EARLY) * (len(ORDER) - 16) < count * (steps - EARLY):
            v_step(done)
            done += 1
    while done < steps:
        v_step(done)
        done += 1
    flag_ref[0, 0] = jnp.where(jnp.max(most) >= SLOTS, 1, 0)
    spread = (my_slot[:, :SLOTS] == lane_i[:, :SLOTS].astype(F32)).astype(BF16)
    pltpu.make_async_copy(g.at[pl.ds(0, 32)], g.at[pl.ds(0, 32)], mate_sem).wait()

    for k in range(CD // 128):
        block = jnp.concatenate([g[((k // 2) * NY + c) * NR + k % 2] for c in range(NX)], axis=0)
        hi, lo = split2(block)
        chi[: NX * SLOTS, k * 128 : (k + 1) * 128] = hi
        chi[NX * SLOTS :, k * 128 : (k + 1) * 128] = lo

    def columns(q):
        return pl.ds(STARTS[q], WIDTHS[q])

    def x_copy(q, d):
        to = (x + d) % NX
        return pltpu.make_async_remote_copy(
            src_ref=part.at[to, :, columns(q)], dst_ref=landed.at[d - 1, :, columns(q)], send_sem=x_send.at[q, d - 1],
            recv_sem=x_recv.at[q, d - 1], device_id=(ab, to), device_id_type=MESH,
        )

    def product(q):
        cols = slice(STARTS[q], STARTS[q] + WIDTHS[q])
        both = dot_nt(chi[...], vhi[cols, :])
        cross = dot_nt(chi[: NX * SLOTS, :], vlo[cols, :])
        total = both[: NX * SLOTS] + both[NX * SLOTS :] + cross
        for c in range(NX):
            part[c, :, cols] = total[c * SLOTS : (c + 1) * SLOTS]
        for d in (2, 1, 3):
            x_copy(q, d).start()

    ab_f = ab_row.astype(F32)

    def exchange(q):
        cols = slice(STARTS[q], STARTS[q] + WIDTHS[q])
        for d in (1, 3, 2):
            x_copy(q, d).wait_recv()
        total = part[x, :, cols] + landed[0, :, cols] + landed[1, :, cols] + landed[2, :, cols]
        hi = total.astype(BF16)
        mid, lo = split2(total - hi.astype(F32))
        rows = dot(spread, hi) + dot(spread, mid) + dot(spread, lo)
        rows = jnp.where(my_label[:, :1] == ab_f[:, cols], rows, 0.0)
        dense[:, :, cols] = rows.reshape(NAB, 4, WIDTHS[q])

        def send(to):
            pltpu.make_async_remote_copy(
                src_ref=dense.at[to, :, columns(q)], dst_ref=out_ref.at[ab, :, columns(q)], send_sem=a_send,
                recv_sem=a_recv, device_id=(to, x), device_id_type=MESH,
            ).start()

        to_all(send)
        out_ref[ab, :, cols] = dense[ab, :, cols]

    product(0)
    for q in range(CHUNKS):
        if q + 1 < CHUNKS:
            product(q + 1)
        exchange(q)

    for q in range(CHUNKS):
        for d in (1, 2, 3):
            x_copy(q, d).wait_send()
    pltpu.make_async_copy(labels.at[others], labels.at[others], s_send.at[0]).wait()
    pltpu.make_async_copy(rows4.at[others], rows4.at[others], s_send.at[1]).wait()
    pltpu.make_async_copy(g.at[others], g.at[others], send_sem).wait()
    pltpu.make_async_copy(out_ref.at[others], out_ref.at[others], a_send).wait()
    pltpu.make_async_copy(out_ref.at[others], out_ref.at[others], a_recv).wait()


def compact(t2_amps, v_slab, ij_irrep, ab_irrep, cd_irrep):
    vmem = pl.BlockSpec(memory_space=pltpu.VMEM)
    hbm = pl.BlockSpec(memory_space=pl.ANY)
    return pl.pallas_call(
        kernel,
        out_shape=(jax.ShapeDtypeStruct((NAB, 4, AB), F32), jax.ShapeDtypeStruct((1, 1), jnp.int32)),
        in_specs=[hbm, hbm, vmem, vmem, vmem, vmem],
        out_specs=(vmem, pl.BlockSpec(memory_space=pltpu.SMEM)),
        scratch_shapes=[
            pltpu.VMEM((ROWS, CD), F32),
            pltpu.VMEM((NAB, 4, 128), F32),
            pltpu.VMEM((1, 128), jnp.int32),
            pltpu.VMEM((NAB, 1, 128), jnp.int32),
            pltpu.VMEM((NAB, 4, 128), F32),
            pltpu.VMEM((NAB, SLOTS, 128), F32),
            pltpu.VMEM((AB // VROWS, VROWS, CD), F32),
            pltpu.VMEM((AB, CD), BF16),
            pltpu.VMEM((AB, CD), BF16),
            pltpu.VMEM((AB, 128), jnp.int32),
            pltpu.VMEM((2 * NX * SLOTS, CD), BF16),
            pltpu.VMEM((NX, SLOTS, AB), F32),
            pltpu.VMEM((NX - 1, SLOTS, AB), F32),
            pltpu.VMEM((NAB, 4, AB), F32),
            pltpu.SemaphoreType.DMA((3,)),
            pltpu.SemaphoreType.DMA((AB // VROWS,)),
            pltpu.SemaphoreType.DMA((2,)),
            pltpu.SemaphoreType.DMA,
            pltpu.SemaphoreType.DMA,
            pltpu.SemaphoreType.DMA((len(ORDER),)),
            pltpu.SemaphoreType.DMA,
            pltpu.SemaphoreType.DMA,
            pltpu.SemaphoreType.DMA((CHUNKS, 3)),
            pltpu.SemaphoreType.DMA((CHUNKS, 3)),
            pltpu.SemaphoreType.DMA,
            pltpu.SemaphoreType.DMA,
        ],
        compiler_params=pltpu.CompilerParams(
            collective_id=0, has_side_effects=True, vmem_limit_bytes=48 * 1024 * 1024
        ),
    )(t2_amps, v_slab, ij_irrep[None, :], ab_irrep[None, :], cd_irrep[None, :], cd_irrep.reshape(CD // 128, 128))


def dense_path(t2_amps, v_slab, ij_irrep, ab_irrep, cd_irrep):
    t2_sym = t2_amps * (ij_irrep[:, None] == cd_irrep[None, :]).astype(F32)
    v_sym = v_slab * (ab_irrep[:, None] == cd_irrep[None, :]).astype(F32)
    gathered = t2_sym
    hop = 1
    while hop < NAB:
        moved = lax.ppermute(gathered, "ab", [(i, (i + hop) % NAB) for i in range(NAB)])
        gathered = jnp.concatenate([moved, gathered], axis=0)
        hop *= 2
    me, x = lax.axis_index("ab"), lax.axis_index("cd")
    gathered = jnp.roll(gathered, (me + 1) * ROWS, axis=0)
    partial = lax.dot_general(
        gathered, v_sym, (((1,), (1,)), ((), ())), precision=lax.Precision.HIGHEST, preferred_element_type=F32
    )
    parts = jnp.transpose(partial.reshape(NAB, NX, ROWS // NX, AB), (1, 0, 2, 3))
    summed = lax.dynamic_index_in_dim(parts, x, 0, keepdims=False)
    for d in range(1, NX):
        theirs = lax.dynamic_index_in_dim(parts, (x + d) % NX, 0, keepdims=False)
        summed = summed + lax.ppermute(theirs, "cd", [(i, (i + d) % NX) for i in range(NX)])
    return lax.all_to_all(summed.reshape(NAB * ROWS // NX, AB), "ab", split_axis=0, concat_axis=1, tiled=True)


def on_device(t2_amps, v_slab, ij_irrep, ab_irrep, cd_irrep):
    rows, over = compact(t2_amps, v_slab, ij_irrep, ab_irrep, cd_irrep)

    def finish(rows, *_):
        return jnp.transpose(rows, (1, 0, 2)).reshape(4, NAB * AB)

    def dense(_, *args):
        return dense_path(*args)

    return lax.cond(
        over[0, 0] > 0, dense, finish, rows, t2_amps, v_slab, ij_irrep, ab_irrep, cd_irrep
    )


def solution(mesh):
    in_specs = (P("ab", "cd"), P("ab", "cd"), P("ab"), P("ab"), P("cd"))
    return jax.shard_map(on_device, mesh=mesh, in_specs=in_specs, out_specs=P(("ab", "cd"), None), check_vma=False)
```
